128 devices in a mesh: chan: 8 (over z, core), sec: 16 (over y, x).
Axes of the slice: x: 4, y: 4, z: 4, core: 2. Of those that a mesh axis runs over, the one named last changes fastest.
Arguments:
- psi: bfloat16 [384, 4, 256, 256], P('sec'), may hold values from -6 to 6
- mpo: float32 [8, 4, 4], P('chan'), may hold values from -1 to 1
- left_env: bfloat16 [8, 128, 256, 256], P('chan', 'sec'), may hold values from -0.375 to 0.375
- right_env: bfloat16 [8, 384, 256, 256], P('chan', 'sec'), may hold values from -0.375 to 0.375
- left_dims: int32 [128], P('sec'), may hold values from 128 to 256, as said below
- right_dims: int32 [384], P('sec'), may hold values from 128 to 256, as said below
- dest_owner: int32 [384, 1], P('sec'), may hold values from 0 to 15, as said below
- left_slot: int32 [384], P('sec'), may hold values from 0 to 7
Outputs:
- h_psi: bfloat16 [384, 4, 256, 256], P('sec', None, 'chan')
The draws below stay inside these ranges and needn't reach their ends.
Inputs may be any that keep to these rules, and one draw needn't show every extreme that they name: `dest_owner`: each device's 24 blocks name one owner at most 2 times; in every draw some owner is named exactly 2 times by the blocks of every device. `left_dims`: multiples of 128; both bounds are reached. `right_dims`: multiples of 128; both bounds are reached.
All inputs are finite; a program needn't handle non-finite values.
Results may differ from the reference program's by a relative error of at most 0.014.
Values may be sent and summed in bfloat16 or wider, within the bound.
A program may use at most 192 MiB of HBM per device.

```python
import jax
import jax.numpy as jnp
from jax import lax

UNIT = 128
B = 256
P_SIZE = 4
BLK_DEV = 24
LSEC_DEV = 8
CAP = 2
NB = 384
LSECT = 128
W = 8
N_CHAN = 8


def draw_widths(key, count):
    units = jax.random.randint(key, (count,), 1, B // UNIT + 1)
    widths = (UNIT * units).astype(jnp.int32)
    return widths.at[0].set(B).at[1].set(UNIT)


def draw_left_dims(key, part):
    return draw_widths(jax.random.fold_in(key, 101), LSECT)


def draw_right_dims(key, part):
    return draw_widths(jax.random.fold_in(key, 202), NB)


def draw_dest_owner(key, part):
    owners = NB // BLK_DEV
    busiest = jax.random.randint(jax.random.fold_in(key, 7), (), 0, owners)
    labels = jnp.repeat(jnp.arange(owners, dtype=jnp.int32), CAP)

    def draw_row(number):
        row_key = jax.random.fold_in(jax.random.fold_in(key, 303), number)
        ranks = jax.random.permutation(row_key, owners * CAP).astype(jnp.int32)
        scores = ranks + jnp.where(labels == busiest, owners * CAP, 0).astype(jnp.int32)
        picked = jnp.argsort(-scores, stable=True)[:BLK_DEV]
        chosen = labels[picked]
        return jax.random.permutation(jax.random.fold_in(row_key, 3), chosen)
    table = jax.vmap(draw_row)(jnp.arange(owners, dtype=jnp.int32))
    return table.reshape(NB, 1).astype(jnp.int32)


def plant(values, own_key, least, largest):
    longest = values.shape.index(max(values.shape))
    spots = []
    for shift in (0, 1):
        where = [jax.random.randint(jax.random.fold_in(own_key, axis), (), 0, length) for axis, length in enumerate(values.shape)]
        where[longest] = (where[longest] + shift) % values.shape[longest]
        spots.append(tuple(where))
    return values.at[spots[0]].set(least).at[spots[1]].set(largest)


def block_levels(stream_key, extent, split, smallest, high):
    loudness, own = 1.0, jax.random.fold_in(stream_key, 6)
    for axis_at, blocks in split:
        steps = jnp.exp(jax.random.uniform(jax.random.fold_in(own, axis_at), (blocks,), jnp.float32, smallest / len(split), high / len(split)))
        loudness = loudness * jnp.repeat(steps, extent[axis_at] // blocks).reshape([-1 if axis == axis_at else 1 for axis in range(len(extent))])
    return loudness


def gaussian(own_key, shape, width, reach, cuts=(), kind=jnp.bfloat16):
    entries = jax.random.normal(own_key, shape, jnp.float32) * width
    if len(cuts) > 0:
        entries = block_levels(own_key, shape, cuts, -0.22, 0.18) * entries
    return jnp.clip(entries, min=-reach, max=reach).astype(kind)


def setup_inputs(seed: int = 0) -> dict:
    key_of = jax.random.split(jax.random.key(seed), 9)
    return {
        "psi": gaussian(key_of[0], (NB, P_SIZE, B, B), 1.0, 6.0, ((0, 16),)),
        "mpo": gaussian(key_of[1], (W, P_SIZE, P_SIZE), (P_SIZE * W) ** -0.5, 1.0, ((0, 8),), jnp.float32),
        "left_env": gaussian(key_of[2], (W, LSECT, B, B), B ** -0.5, 0.375, ((0, 8), (1, 16))),
        "right_env": gaussian(key_of[3], (W, NB, B, B), B ** -0.5, 0.375, ((0, 8), (1, 16))),
        "left_dims": draw_left_dims(jax.random.fold_in(key_of[8], 71), 0),
        "right_dims": draw_right_dims(jax.random.fold_in(key_of[8], 71), 0),
        "dest_owner": draw_dest_owner(jax.random.fold_in(key_of[8], 71), 0),
        "left_slot": plant(jax.random.randint(key_of[7], (NB,), 0, LSEC_DEV), jax.random.fold_in(key_of[7], 1), 0, LSEC_DEV - 1).astype(jnp.int32),
    }


def reference(psi, mpo, left_env, right_env, left_dims, right_dims, dest_owner, left_slot):
    places = jnp.arange(B, dtype=jnp.int32)
    left_mask = (places[None, :] < left_dims[:, None]).astype(jnp.bfloat16)
    right_mask = (places[None, :] < right_dims[:, None]).astype(jnp.bfloat16)
    sector_of = (dest_owner[:, 0] * LSEC_DEV + left_slot).astype(jnp.int32)

    def per_block(block_index):
        current = psi[block_index].astype(jnp.float32)
        sector = sector_of[block_index]
        left_row = left_mask[sector]
        right_row = right_mask[block_index]
        summed = jnp.zeros((P_SIZE, B, B), jnp.float32)
        for channel in range(N_CHAN):
            right_kept = right_env[channel, block_index] * (right_row[:, None] * right_row[None, :])
            left_kept = left_env[channel, sector] * (left_row[:, None] * left_row[None, :])
            inner = jnp.einsum('pac,dc->pad', current, right_kept.astype(jnp.float32))
            mixed = jnp.einsum('sp,pad->sad', mpo[channel], inner, precision=lax.Precision.HIGHEST)
            mixed = lax.optimization_barrier(mixed.astype(jnp.bfloat16)).astype(jnp.float32)
            product = jnp.einsum('ea,sad->sed', left_kept.astype(jnp.float32), mixed)
            product = lax.optimization_barrier(product.astype(jnp.bfloat16)).astype(jnp.float32)
            summed = summed + product
        return summed.astype(jnp.bfloat16)

    return lax.map(per_block, jnp.arange(NB, dtype=jnp.int32))
```

```python
import jax
import jax.numpy as jnp
from jax import lax
from jax.sharding import PartitionSpec as P


def on_device(psi, mpo, left_env, right_env, left_dims, right_dims, dest_owner, left_slot):
    block_width = psi.shape[2]
    blocks = psi.shape[0]
    owners = lax.axis_size("sec")
    capacity = max(2, (blocks + owners - 1) // owners)
    places = jnp.arange(block_width, dtype=jnp.int32)
    right_mask = (places[None, :] < right_dims[:, None]).astype(jnp.bfloat16)
    left_mask = (places[None, :] < left_dims[:, None]).astype(jnp.bfloat16)
    target = dest_owner[:, 0]
    marks = (target[:, None] == jnp.arange(owners, dtype=jnp.int32)[None, :]).astype(jnp.int32)
    position = jnp.sum(jnp.cumsum(marks, axis=0) * marks, axis=1) - 1
    slot_of = target * capacity + position
    here = slot_of[:, None] == jnp.arange(owners * capacity, dtype=jnp.int32)[None, :]
    wanted = jnp.sum(jnp.where(here, left_slot[:, None], 0), axis=0)
    asked = lax.all_to_all(
        wanted.reshape(owners, capacity), "sec", split_axis=0, concat_axis=0, tiled=True
    )
    left_kept = left_env[0] * (left_mask[:, :, None] * left_mask[:, None, :])
    outbound = jnp.take(left_kept, asked, axis=0, mode="clip")
    arrived = lax.all_to_all(outbound, "sec", split_axis=0, concat_axis=0, tiled=True)
    right_kept = right_env[0] * (right_mask[:, :, None] * right_mask[:, None, :])
    inner = jnp.einsum("kpac,kdc->kpad", psi, right_kept, preferred_element_type=jnp.float32)
    mixed = jnp.einsum("sp,kpad->ksad", mpo[0], inner, precision=lax.Precision.HIGHEST).astype(
        jnp.bfloat16
    )
    picked = jnp.take(
        arrived.reshape((owners * capacity,) + arrived.shape[2:]), slot_of, axis=0, mode="clip"
    )
    product = jnp.einsum("kea,ksad->ksed", picked, mixed, preferred_element_type=jnp.float32)
    return lax.psum_scatter(
        product.astype(jnp.bfloat16), "chan", scatter_dimension=2, tiled=True
    )


def solution(mesh):
    in_specs = (
        P("sec", None, None, None),
        P("chan", None, None),
        P("chan", "sec", None, None),
        P("chan", "sec", None, None),
        P("sec"),
        P("sec"),
        P("sec", None),
        P("sec"),
    )
    out_specs = P("sec", None, "chan", None)
    return jax.shard_map(
        on_device, mesh=mesh, in_specs=in_specs, out_specs=out_specs, check_vma=False
    )
```

```python
import functools

import jax
import jax.numpy as jnp
from jax import lax
from jax.experimental import pallas as pl
from jax.experimental.pallas import tpu as pltpu
from jax.sharding import PartitionSpec as P

MESH = pl.DeviceIdType.MESH
F32 = jnp.float32
BF16 = jnp.bfloat16

Z = 4
SIDE = 4
OWNERS = SIDE * SIDE
CAP = 2
PHASES = Z
GROUPS = 4
EARLY = 6
OFFSETS = [(dx, dy) for dx in range(SIDE) for dy in range(SIDE) if dx or dy]


def kernel(
    mpo, left_dims, right_dims, dest, slot, left_ref, psi_hbm, right_hbm, out_ref,
    left_kept, table, tables, table_smem, slot_smem, stage, arr0, arr1, arr2, arr3,
    mixed, psi_buf, right_buf, mine, give0, give1, give2, give3, got0, got1, got2, got3,
    ring_out0, ring_out1, ring_out2, ring_in0, ring_in1, ring_in2,
    tab_send, tab_recv, tab_local, a_send, a_recv, p_sem, r_sem, g_send, g_recv, n_send, n_recv,
):
    blocks, states, width = psi_hbm.shape[0], psi_hbm.shape[1], psi_hbm.shape[2]
    sectors = left_ref.shape[1]
    rows = width // (2 * Z)
    per = blocks // GROUPS
    arrived = (arr0, arr1, arr2, arr3)
    give = (give0, give1, give2, give3)
    got = (got0, got1, got2, got3)
    ring_out = (ring_out0, ring_out1, ring_out2)
    ring_in = (ring_in0, ring_in1, ring_in2)

    chan = lax.axis_index("chan")
    me = lax.axis_index("sec")
    z, core = chan // 2, lax.rem(chan, 2)
    y, x = me // SIDE, lax.rem(me, SIDE)
    up = lax.rem(z + 1 + 2 * core, Z) * 2 + core
    down = lax.rem(z + 3 + 2 * core, Z) * 2 + core
    partner = z * 2 + 1 - core

    def away(dx, dy):
        return lax.rem(y + dy, SIDE) * SIDE + lax.rem(x + dx, SIDE)

    barrier = pltpu.get_barrier_semaphore()
    for dx, dy in OFFSETS:
        pl.semaphore_signal(barrier, inc=1, device_id=(chan, away(dx, dy)), device_id_type=MESH)
    for other in (down, partner):
        pl.semaphore_signal(barrier, inc=1, device_id=(other, me), device_id_type=MESH)

    def fetch(k, b):
        pltpu.make_async_copy(psi_hbm.at[k], psi_buf.at[b], p_sem.at[b]).start()
        pltpu.make_async_copy(right_hbm.at[0, k], right_buf.at[b], r_sem.at[b]).start()

    fetch(0, 0)

    lane = lax.broadcasted_iota(jnp.int32, (1, 128), 1)
    lane_owner, lane_place = lane // CAP, lax.rem(lane, CAP)
    wanted = jnp.zeros((1, 128), jnp.int32)
    count = jnp.zeros((1, 128), jnp.int32)
    for k in range(blocks):
        own = lane_owner == dest[k, 0]
        wanted = jnp.where(own & (count == lane_place), slot[k], wanted)
        count = count + jnp.where(own, 1, 0)
    table[...] = wanted

    for k in range(blocks):
        place = dest[k, 0] * CAP
        for before in range(k):
            place = place + jnp.where(dest[before, 0] == dest[k, 0], 1, 0)
        slot_smem[k] = place

    row_at = lax.broadcasted_iota(jnp.int32, (width, width), 0)
    col_at = lax.broadcasted_iota(jnp.int32, (width, width), 1)

    def kept(values, dim):
        mask = jnp.where((row_at < dim) & (col_at < dim), 1.0, 0.0).astype(BF16)
        return values * mask

    def keep_left(s, _):
        left_kept[s] = kept(left_ref[0, s], left_dims[s])
        return 0

    lax.fori_loop(0, sectors, keep_left, 0)

    pl.semaphore_wait(barrier, len(OFFSETS) + 2)

    asks = []
    for o, (dx, dy) in enumerate(OFFSETS):
        asks.append(
            pltpu.make_async_remote_copy(
                src_ref=table, dst_ref=tables.at[o], send_sem=tab_send.at[o],
                recv_sem=tab_recv.at[o], device_id=(chan, away(dx, dy)), device_id_type=MESH,
            )
        )
        asks[-1].start()
    tables[OWNERS - 1] = wanted

    def mix(k, _):
        b = lax.rem(k, 2)

        @pl.when(k + 1 < blocks)
        def _():
            fetch(k + 1, 1 - b)

        pltpu.make_async_copy(psi_hbm.at[k], psi_buf.at[b], p_sem.at[b]).wait()
        pltpu.make_async_copy(right_hbm.at[0, k], right_buf.at[b], r_sem.at[b]).wait()
        right = kept(right_buf[b], right_dims[k])
        inner = lax.dot_general(
            psi_buf[b].reshape(states * width, width), right, (((1,), (1,)), ((), ())),
            preferred_element_type=F32,
        )
        for s in range(states):
            total = mpo[0, s, 0] * inner[:width]
            for p in range(1, states):
                total = total + mpo[0, s, p] * inner[p * width : (p + 1) * width]
            mixed[k, :, s * width : (s + 1) * width] = total.astype(BF16)
        return 0

    lax.fori_loop(0, EARLY, mix, 0)

    for ask in asks:
        ask.wait_recv()
    local = pltpu.make_async_copy(tables, table_smem, tab_local)
    local.start()
    local.wait()

    def first_row(p, c):
        chip = jnp.where(c == 0, lax.rem(z + 3 - p + Z, Z), lax.rem(z + 1 + p, Z))
        return pl.multiple_of((chip * 2 + c) * rows, rows)

    sends = []
    for p in range(PHASES):
        own_row, other_row = first_row(p, core), first_row(p, 1 - core)

        def put(o, _, own_row=own_row, other_row=other_row, p=p):
            for q in range(CAP):
                s = table_smem[o, 0, CAP * me + q]
                stage[p, o, q, :rows] = left_kept[s, pl.ds(own_row, rows), :]
                stage[p, o, q, rows:] = left_kept[s, pl.ds(other_row, rows), :]
            return 0

        lax.fori_loop(0, OWNERS - 1, put, 0)
        for o, (dx, dy) in enumerate(OFFSETS):
            sends.append(
                pltpu.make_async_remote_copy(
                    src_ref=stage.at[p, o], dst_ref=arrived[p].at[pl.ds(CAP * me, CAP)],
                    send_sem=a_send.at[p, o], recv_sem=a_recv.at[p, o],
                    device_id=(chan, away(SIDE - dx, SIDE - dy)), device_id_type=MESH,
                )
            )
            sends[-1].start()
        for q in range(CAP):
            s = table_smem[OWNERS - 1, 0, CAP * me + q]
            arrived[p][CAP * me + q, :rows] = left_kept[s, pl.ds(own_row, rows), :]
            arrived[p][CAP * me + q, rows:] = left_kept[s, pl.ds(other_row, rows), :]

    lax.fori_loop(EARLY, blocks, mix, 0)

    others = []

    def apply_left(p, g):
        def one(k, _):
            term = jnp.dot(arrived[p][slot_smem[k]], mixed[k], preferred_element_type=F32)
            mine[k] = term[:rows]
            give[p][k] = term[rows:].astype(BF16)
            return 0

        lax.fori_loop(g * per, (g + 1) * per, one, 0)
        part = pl.ds(g * per, per)
        copy = pltpu.make_async_remote_copy(
            src_ref=give[p].at[part], dst_ref=got[p].at[part], send_sem=g_send.at[p, g],
            recv_sem=g_recv.at[p, g], device_id=(partner, me), device_id_type=MESH,
        )
        copy.start()
        others.append(copy)
        return copy

    hops = {}

    def combine(p, g, copy):
        copy.wait_recv()
        if p:
            hops[p - 1, g].wait_recv()

        def one(k, _):
            total = mine[k] + got[p][k].astype(F32)
            if p:
                total = total + ring_in[p - 1][k].astype(F32)
            total = total.astype(BF16)
            if p < PHASES - 1:
                ring_out[p][k] = total
            else:
                for s in range(states):
                    out_ref[k, s] = total[:, s * width : (s + 1) * width]
            return 0

        lax.fori_loop(g * per, (g + 1) * per, one, 0)
        if p < PHASES - 1:
            part = pl.ds(g * per, per)
            hops[p, g] = pltpu.make_async_remote_copy(
                src_ref=ring_out[p].at[part], dst_ref=ring_in[p].at[part],
                send_sem=n_send.at[p, g], recv_sem=n_recv.at[p, g],
                device_id=(up, me), device_id_type=MESH,
            )
            hops[p, g].start()

    for p in range(PHASES):
        for o in range(OWNERS - 1):
            sends[p * (OWNERS - 1) + o].wait_recv()
        copies = []
        for g in range(GROUPS):
            copies.append(apply_left(p, g))
            if g:
                combine(p, g - 1, copies[g - 1])
        combine(p, GROUPS - 1, copies[GROUPS - 1])

    for copy in asks + sends + others + list(hops.values()):
        copy.wait_send()


def on_device(psi, mpo, left_env, right_env, left_dims, right_dims, dest_owner, left_slot):
    blocks, states, width = psi.shape[0], psi.shape[1], psi.shape[2]
    sectors = left_env.shape[1]
    rows = width // (2 * Z)
    wide = states * width
    smem = pl.BlockSpec(memory_space=pltpu.SMEM)
    vmem = pl.BlockSpec(memory_space=pltpu.VMEM)
    hbm = pl.BlockSpec(memory_space=pl.ANY)
    dma = pltpu.SemaphoreType.DMA
    piece = pltpu.VMEM((blocks, rows, wide), BF16)
    return pl.pallas_call(
        kernel,
        out_shape=jax.ShapeDtypeStruct((blocks, states, rows, width), BF16),
        in_specs=[smem] * 5 + [vmem, hbm, hbm],
        out_specs=vmem,
        scratch_shapes=[
            pltpu.VMEM((sectors, width, width), BF16),
            pltpu.VMEM((1, 128), jnp.int32),
            pltpu.VMEM((OWNERS, 1, 128), jnp.int32),
            pltpu.SMEM((OWNERS, 1, 128), jnp.int32),
            pltpu.SMEM((blocks,), jnp.int32),
            pltpu.VMEM((PHASES, OWNERS - 1, CAP, 2 * rows, width), BF16),
            *[pltpu.VMEM((OWNERS * CAP, 2 * rows, width), BF16)] * PHASES,
            pltpu.VMEM((blocks, width, wide), BF16),
            pltpu.VMEM((2, states, width, width), BF16),
            pltpu.VMEM((2, width, width), BF16),
            pltpu.VMEM((blocks, rows, wide), F32),
            *[piece] * (2 * PHASES + 2 * (PHASES - 1)),
            dma((OWNERS - 1,)),
            dma((OWNERS - 1,)),
            dma,
            dma((PHASES, OWNERS - 1)),
            dma((PHASES, OWNERS - 1)),
            dma((2,)),
            dma((2,)),
            dma((PHASES, GROUPS)),
            dma((PHASES, GROUPS)),
            dma((PHASES - 1, GROUPS)),
            dma((PHASES - 1, GROUPS)),
        ],
        compiler_params=pltpu.CompilerParams(
            collective_id=0, has_side_effects=True, vmem_limit_bytes=67043328
        ),
    )(mpo, left_dims, right_dims, dest_owner, left_slot, left_env, psi, right_env)


def solution(mesh):
    in_specs = (
        P("sec", None, None, None),
        P("chan", None, None),
        P("chan", "sec", None, None),
        P("chan", "sec", None, None),
        P("sec"),
        P("sec"),
        P("sec", None),
        P("sec"),
    )
    out_specs = P("sec", None, "chan", None)
    return jax.shard_map(
        on_device, mesh=mesh, in_specs=in_specs, out_specs=out_specs, check_vma=False
    )
```

```python
import functools

import jax
import jax.numpy as jnp
from jax import lax
from jax.experimental import pallas as pl
from jax.experimental.pallas import tpu as pltpu
from jax.sharding import PartitionSpec as P

MESH = pl.DeviceIdType.MESH
F32 = jnp.float32
BF16 = jnp.bfloat16

Z = 4
SIDE = 4
OWNERS = SIDE * SIDE
CAP = 2
PHASES = Z
GROUPS = 4
PSI_READ = 2
RIGHT_READ = 4
ASKING = 5
ALONE = 7
BEFORE = 14
CHUNKS = ((0, 0, 16), (0, 16, 16), (1, 0, 32), (2, 0, 32), (3, 0, 32))
OFFSETS = (
    (1, 0), (0, 1), (3, 0), (0, 3), (1, 1), (3, 3), (1, 3), (3, 1),
    (2, 0), (0, 2), (2, 1), (1, 2), (2, 3), (3, 2), (2, 2),
)


def kernel(
    mpo, left_dims, right_dims, dest, slot, left_hbm, psi_hbm, right_hbm, out_hbm,
    left_kept, table, tables, table_smem, slot_smem,
    stage0, stage1, stage2, stage3, stage4, arr0, arr1, arr2, arr3, arr4,
    work, right_all, mine, give0, give1, give2, give3, got0, got1, got2, got3,
    ring_out0, ring_out1, ring_out2, ring_in0, ring_in1, ring_in2, out_buf,
    tab_send, tab_recv, tab_local, a_send, a_recv, p_sem, r_sem, l_sem, o_sem,
    g_send, g_recv, n_send, n_recv,
):
    blocks, states, width = psi_hbm.shape[0], psi_hbm.shape[1], psi_hbm.shape[2]
    sectors = left_kept.shape[0]
    rows = width // (2 * Z)
    per = blocks // GROUPS
    stage = (stage0, stage1, stage2, stage3, stage4)
    arrived = (arr0, arr1, arr2, arr3, arr4)
    give = (give0, give1, give2, give3)
    got = (got0, got1, got2, got3)
    ring_out = (ring_out0, ring_out1, ring_out2)
    ring_in = (ring_in0, ring_in1, ring_in2)

    chan = lax.axis_index("chan")
    me = lax.axis_index("sec")
    z, core = chan // 2, lax.rem(chan, 2)
    y, x = me // SIDE, lax.rem(me, SIDE)
    up = lax.rem(z + 1 + 2 * core, Z) * 2 + core
    down = lax.rem(z + 3 + 2 * core, Z) * 2 + core
    partner = z * 2 + 1 - core

    def away(dx, dy):
        return lax.rem(y + dy, SIDE) * SIDE + lax.rem(x + dx, SIDE)

    barrier = pltpu.get_barrier_semaphore()
    for dx, dy in OFFSETS:
        pl.semaphore_signal(barrier, inc=1, device_id=(chan, away(dx, dy)), device_id_type=MESH)
    for other in (down, partner):
        pl.semaphore_signal(barrier, inc=1, device_id=(other, me), device_id_type=MESH)

    def psi_copy(i):
        part = pl.ds(i * PSI_READ, PSI_READ)
        return pltpu.make_async_copy(psi_hbm.at[part], work.at[part], p_sem.at[i])

    def right_copy(i):
        part = pl.ds(i * RIGHT_READ, RIGHT_READ)
        return pltpu.make_async_copy(right_hbm.at[0, part], right_all.at[part], r_sem.at[i])

    def all_of(ref, sem):
        return pltpu.make_async_copy(ref, ref, sem)

    left_copy = pltpu.make_async_copy(left_hbm.at[0], left_kept, l_sem)

    def read(first, last):
        for k in range(first, last):
            if k % RIGHT_READ == 0:
                right_copy(k // RIGHT_READ).start()
            if k % PSI_READ == 0:
                psi_copy(k // PSI_READ).start()

    read(0, ASKING)
    left_copy.start()

    lane = lax.broadcasted_iota(jnp.int32, (1, 128), 1)
    lane_owner, lane_place = lane // CAP, lax.rem(lane, CAP)
    wanted = jnp.zeros((1, 128), jnp.int32)
    count = jnp.zeros((1, 128), jnp.int32)
    for k in range(blocks):
        own = lane_owner == dest[k]
        wanted = jnp.where(own & (count == lane_place), slot[k], wanted)
        count = count + jnp.where(own, 1, 0)
    table[...] = wanted

    pl.semaphore_wait(barrier, len(OFFSETS) + 2)

    for o, (dx, dy) in enumerate(OFFSETS):
        pltpu.make_async_remote_copy(
            src_ref=table, dst_ref=tables.at[o], send_sem=tab_send, recv_sem=tab_recv,
            device_id=(chan, away(dx, dy)), device_id_type=MESH,
        ).start()
    tables[OWNERS - 1] = wanted
    read(ASKING, blocks)

    row_at = lax.broadcasted_iota(jnp.int32, (width, width), 0)
    col_at = lax.broadcasted_iota(jnp.int32, (width, width), 1)

    def kept(values, dim):
        mask = jnp.where((row_at < dim) & (col_at < dim), 1.0, 0.0).astype(BF16)
        return values * mask

    def mix(k, _):
        @pl.when(lax.rem(k, RIGHT_READ) == 0)
        def _():
            right_copy(k // RIGHT_READ).wait()

        @pl.when(lax.rem(k, PSI_READ) == 0)
        def _():
            psi_copy(k // PSI_READ).wait()

        right = kept(right_all[k], right_dims[k])
        inner = lax.dot_general(
            work[k].reshape(states * width, width), right, (((1,), (1,)), ((), ())),
            preferred_element_type=F32,
        )
        for s in range(states):
            total = mpo[0, s, 0] * inner[:width]
            for p in range(1, states):
                total = total + mpo[0, s, p] * inner[p * width : (p + 1) * width]
            work[k, s] = total.astype(BF16)
        return 0

    def keep_left(s, _):
        left_kept[s] = kept(left_kept[s], left_dims[s])
        return 0

    lax.fori_loop(0, ASKING, mix, 0)
    left_copy.wait()
    lax.fori_loop(0, sectors, keep_left, 0)

    all_of(tables.at[pl.ds(0, OWNERS - 1)], tab_recv).wait()
    local = pltpu.make_async_copy(tables, table_smem, tab_local)
    local.start()

    for k in range(blocks):
        place = dest[k] * CAP
        for before in range(k):
            place = place + jnp.where(dest[before] == dest[k], 1, 0)
        slot_smem[k] = place

    local.wait()

    def first_row(p, c):
        chip = jnp.where(c == 0, lax.rem(z + 3 - p + Z, Z), lax.rem(z + 1 + p, Z))
        return (chip * 2 + c) * rows

    def issue(c):
        p, first, num = CHUNKS[c]
        own_row = pl.multiple_of(first_row(p, core) + first, 16)
        other_row = pl.multiple_of(first_row(p, 1 - core) + first, 16)

        def put(o, _):
            for q in range(CAP):
                s = table_smem[o, 0, CAP * me + q]
                stage[c][o, q, :num] = left_kept[s, pl.ds(own_row, num), :]
                stage[c][o, q, num:] = left_kept[s, pl.ds(other_row, num), :]
            return 0

        lax.fori_loop(0, OWNERS - 1, put, 0)
        for o, (dx, dy) in enumerate(OFFSETS):
            pltpu.make_async_remote_copy(
                src_ref=stage[c].at[o], dst_ref=arrived[c].at[pl.ds(CAP * me, CAP)],
                send_sem=a_send.at[c], recv_sem=a_recv.at[c],
                device_id=(chan, away(SIDE - dx, SIDE - dy)), device_id_type=MESH,
            ).start()
        for q in range(CAP):
            s = table_smem[OWNERS - 1, 0, CAP * me + q]
            arrived[c][CAP * me + q, :num] = left_kept[s, pl.ds(own_row, num), :]
            arrived[c][CAP * me + q, num:] = left_kept[s, pl.ds(other_row, num), :]

    issue(0)
    lax.fori_loop(ASKING, ASKING + ALONE, mix, 0)
    issue(1)
    lax.fori_loop(ASKING + ALONE, ASKING + BEFORE, mix, 0)
    issue(2)

    hops, outs = {}, []

    def apply_left(c, g):
        p, first, num = CHUNKS[c]

        def one(k, _):
            lhs = arrived[c][slot_smem[k]]
            for s in range(states):
                term = jnp.dot(lhs, work[k, s], preferred_element_type=F32)
                cols = slice(s * width, (s + 1) * width)
                mine[k, first : first + num, cols] = term[:num]
                give[p][k, first : first + num, cols] = term[num:].astype(BF16)
            return 0

        lax.fori_loop(g * per, (g + 1) * per, one, 0)
        part = (pl.ds(g * per, per), pl.ds(first, num))
        copy = pltpu.make_async_remote_copy(
            src_ref=give[p].at[part], dst_ref=got[p].at[part], send_sem=g_send.at[p],
            recv_sem=g_recv.at[c, g], device_id=(partner, me), device_id_type=MESH,
        )
        copy.start()
        return copy

    def combine(c, g, copy):
        p, first, num = CHUNKS[c]
        copy.wait_recv()
        for before, (q, _, _) in enumerate(CHUNKS):
            if q == p - 1:
                hops[before, g].wait_recv()
        at = slice(first, first + num)

        def one(k, _):
            total = mine[k, at] + got[p][k, at].astype(F32)
            if p:
                total = total + ring_in[p - 1][k, at].astype(F32)
            total = total.astype(BF16)
            if p < PHASES - 1:
                ring_out[p][k, at] = total
            else:
                for s in range(states):
                    out_buf[k, s, at] = total[:, s * width : (s + 1) * width]
            return 0

        lax.fori_loop(g * per, (g + 1) * per, one, 0)
        blocks_of = pl.ds(g * per, per)
        if p < PHASES - 1:
            part = (blocks_of, pl.ds(first, num))
            hops[c, g] = pltpu.make_async_remote_copy(
                src_ref=ring_out[p].at[part], dst_ref=ring_in[p].at[part],
                send_sem=n_send.at[p], recv_sem=n_recv.at[c, g],
                device_id=(up, me), device_id_type=MESH,
            )
            hops[c, g].start()
        else:
            outs.append(
                pltpu.make_async_copy(out_buf.at[blocks_of], out_hbm.at[blocks_of], o_sem.at[g])
            )
            outs[-1].start()

    for c in range(len(CHUNKS)):
        all_of(stage[c], a_recv.at[c]).wait()
        if c == 2:
            issue(4)
        copies = []
        for g in range(GROUPS):
            if c == 0 and g == 2:
                lax.fori_loop(ASKING + BEFORE, blocks, mix, 0)
                issue(3)
            copies.append(apply_left(c, g))
            if g:
                combine(c, g - 1, copies[g - 1])
        combine(c, GROUPS - 1, copies[GROUPS - 1])

    all_of(tables.at[pl.ds(0, OWNERS - 1)], tab_send).wait()
    for c in range(len(CHUNKS)):
        all_of(stage[c], a_send.at[c]).wait()
    for p in range(PHASES):
        all_of(give[p], g_send.at[p]).wait()
    for p in range(PHASES - 1):
        all_of(ring_out[p], n_send.at[p]).wait()
    for copy in outs:
        copy.wait()


def on_device(psi, mpo, left_env, right_env, left_dims, right_dims, dest_owner, left_slot):
    blocks, states, width = psi.shape[0], psi.shape[1], psi.shape[2]
    sectors = left_env.shape[1]
    rows = width // (2 * Z)
    wide = states * width
    chunks = len(CHUNKS)
    smem = pl.BlockSpec(memory_space=pltpu.SMEM)
    hbm = pl.BlockSpec(memory_space=pl.ANY)
    dma = pltpu.SemaphoreType.DMA
    piece = pltpu.VMEM((blocks, rows, wide), BF16)
    return pl.pallas_call(
        kernel,
        out_shape=jax.ShapeDtypeStruct((blocks, states, rows, width), BF16),
        in_specs=[smem] * 5 + [hbm] * 3,
        out_specs=hbm,
        scratch_shapes=[
            pltpu.VMEM((sectors, width, width), BF16),
            pltpu.VMEM((1, 128), jnp.int32),
            pltpu.VMEM((OWNERS, 1, 128), jnp.int32),
            pltpu.SMEM((OWNERS, 1, 128), jnp.int32),
            pltpu.SMEM((blocks,), jnp.int32),
            *[pltpu.VMEM((OWNERS - 1, CAP, 2 * num, width), BF16) for _, _, num in CHUNKS],
            *[pltpu.VMEM((OWNERS * CAP, 2 * num, width), BF16) for _, _, num in CHUNKS],
            pltpu.VMEM((blocks, states, width, width), BF16),
            pltpu.VMEM((blocks, width, width), BF16),
            pltpu.VMEM((blocks, rows, wide), F32),
            *[piece] * (2 * PHASES + 2 * (PHASES - 1)),
            pltpu.VMEM((blocks, states, rows, width), BF16),
            dma,
            dma,
            dma,
            dma((chunks,)),
            dma((chunks,)),
            dma((blocks // PSI_READ,)),
            dma((blocks // RIGHT_READ,)),
            dma,
            dma((GROUPS,)),
            dma((PHASES,)),
            dma((chunks, GROUPS)),
            dma((PHASES - 1,)),
            dma((chunks - 1, GROUPS)),
        ],
        compiler_params=pltpu.CompilerParams(
            collective_id=0, has_side_effects=True, vmem_limit_bytes=67043328
        ),
    )(mpo, left_dims, right_dims, dest_owner.reshape(blocks), left_slot, left_env, psi, right_env)


def solution(mesh):
    in_specs = (
        P("sec", None, None, None),
        P("chan", None, None),
        P("chan", "sec", None, None),
        P("chan", "sec", None, None),
        P("sec"),
        P("sec"),
        P("sec", None),
        P("sec"),
    )
    out_specs = P("sec", None, "chan", None)
    return jax.shard_map(
        on_device, mesh=mesh, in_specs=in_specs, out_specs=out_specs, check_vma=False
    )
```

```python
import functools

import jax
import jax.numpy as jnp
from jax import lax
from jax.experimental import pallas as pl
from jax.experimental.pallas import tpu as pltpu
from jax.sharding import PartitionSpec as P

MESH = pl.DeviceIdType.MESH
F32 = jnp.float32
BF16 = jnp.bfloat16

Z = 4
SIDE = 4
OWNERS = SIDE * SIDE
CAP = 2
PHASES = Z
GROUPS = 4
PSI_READ = 2
RIGHT_READ = 4
ASKING = 5
ALONE = 7
BEFORE = 16
CHUNKS = ((0, 0, 16), (0, 16, 16), (1, 0, 32), (2, 0, 32), (3, 0, 32))
OFFSETS = (
    (1, 0), (0, 1), (3, 0), (0, 3), (1, 1), (3, 3), (1, 3), (3, 1),
    (2, 0), (0, 2), (2, 1), (1, 2), (2, 3), (3, 2), (2, 2),
)


def kernel(
    mpo, left_dims, right_dims, dest, slot, left_hbm, psi_hbm, right_hbm, out_ref,
    left_kept, table, asked, slot_smem,
    stage0, stage1, stage2, stage3, stage4, arr0, arr1, arr2, arr3, arr4,
    work, right_all, mine, give0, give1, give2, give3, got0, got1, got2, got3,
    ring_out0, ring_out1, ring_out2, ring_in0, ring_in1, ring_in2,
    tab_send, tab_recv, tab_local, a_send, a_recv, p_sem, r_sem, l_sem,
    g_send, g_recv, n_send, n_recv,
):
    blocks, states, width = psi_hbm.shape[0], psi_hbm.shape[1], psi_hbm.shape[2]
    sectors = left_kept.shape[0]
    rows = width // (2 * Z)
    per = blocks // GROUPS
    stage = (stage0, stage1, stage2, stage3, stage4)
    arrived = (arr0, arr1, arr2, arr3, arr4)
    give = (give0, give1, give2, give3)
    got = (got0, got1, got2, got3)
    ring_out = (ring_out0, ring_out1, ring_out2)
    ring_in = (ring_in0, ring_in1, ring_in2)

    chan = lax.axis_index("chan")
    me = lax.axis_index("sec")
    z, core = chan // 2, lax.rem(chan, 2)
    y, x = me // SIDE, lax.rem(me, SIDE)
    up = lax.rem(z + 1 + 2 * core, Z) * 2 + core
    down = lax.rem(z + 3 + 2 * core, Z) * 2 + core
    partner = z * 2 + 1 - core

    def away(dx, dy):
        return lax.rem(y + dy, SIDE) * SIDE + lax.rem(x + dx, SIDE)

    barrier = pltpu.get_barrier_semaphore()
    for dx, dy in OFFSETS:
        pl.semaphore_signal(barrier, inc=1, device_id=(chan, away(dx, dy)), device_id_type=MESH)
    for other in (down, partner):
        pl.semaphore_signal(barrier, inc=1, device_id=(other, me), device_id_type=MESH)

    def psi_copy(i):
        part = pl.ds(i * PSI_READ, PSI_READ)
        return pltpu.make_async_copy(psi_hbm.at[part], work.at[part], p_sem.at[i])

    def right_copy(i):
        part = pl.ds(i * RIGHT_READ, RIGHT_READ)
        return pltpu.make_async_copy(right_hbm.at[0, part], right_all.at[part], r_sem.at[i])

    def all_of(ref, sem):
        return pltpu.make_async_copy(ref, ref, sem)

    left_copy = pltpu.make_async_copy(left_hbm.at[0], left_kept, l_sem)

    def read(first, last):
        for k in range(first, last):
            if k % RIGHT_READ == 0:
                right_copy(k // RIGHT_READ).start()
            if k % PSI_READ == 0:
                psi_copy(k // PSI_READ).start()

    read(0, ASKING)
    left_copy.start()

    lane = lax.broadcasted_iota(jnp.int32, (1, 128), 1)
    lane_owner, lane_place = lane // CAP, lax.rem(lane, CAP)
    wanted = jnp.zeros((1, 128), jnp.int32)
    count = jnp.zeros((1, 128), jnp.int32)
    for k in range(blocks):
        own = lane_owner == dest[k]
        wanted = jnp.where(own & (count == lane_place), slot[k], wanted)
        count = count + jnp.where(own, 1, 0)
    table[...] = wanted

    pl.semaphore_wait(barrier, len(OFFSETS) + 2)

    for o, (dx, dy) in enumerate(OFFSETS):
        pltpu.make_async_remote_copy(
            src_ref=table, dst_ref=asked.at[o], send_sem=tab_send, recv_sem=tab_recv,
            device_id=(chan, away(dx, dy)), device_id_type=MESH,
        ).start()
    own_ask = pltpu.make_async_copy(table, asked.at[OWNERS - 1], tab_local)
    own_ask.start()
    read(ASKING, blocks)

    row_at = lax.broadcasted_iota(jnp.int32, (width, width), 0)
    col_at = lax.broadcasted_iota(jnp.int32, (width, width), 1)

    def kept(values, dim):
        mask = jnp.where((row_at < dim) & (col_at < dim), 1.0, 0.0).astype(BF16)
        return values * mask

    def mix(k, _):
        @pl.when(lax.rem(k, RIGHT_READ) == 0)
        def _():
            right_copy(k // RIGHT_READ).wait()

        @pl.when(lax.rem(k, PSI_READ) == 0)
        def _():
            psi_copy(k // PSI_READ).wait()

        right = kept(right_all[k], right_dims[k])
        inner = lax.dot_general(
            work[k].reshape(states * width, width), right, (((1,), (1,)), ((), ())),
            preferred_element_type=F32,
        )
        for s in range(states):
            total = mpo[0, s, 0] * inner[:width]
            for p in range(1, states):
                total = total + mpo[0, s, p] * inner[p * width : (p + 1) * width]
            work[k, s] = total.astype(BF16)
        return 0

    def keep_left(s, _):
        left_kept[s] = kept(left_kept[s], left_dims[s])
        return 0

    lax.fori_loop(0, ASKING, mix, 0)
    left_copy.wait()
    lax.fori_loop(0, sectors, keep_left, 0)

    all_of(asked.at[pl.ds(0, OWNERS - 1)], tab_recv).wait()

    for k in range(blocks):
        place = dest[k] * CAP
        for before in range(k):
            place = place + jnp.where(dest[before] == dest[k], 1, 0)
        slot_smem[k] = place

    own_ask.wait()

    def first_row(p, c):
        chip = jnp.where(c == 0, lax.rem(z + 3 - p + Z, Z), lax.rem(z + 1 + p, Z))
        return (chip * 2 + c) * rows

    def issue(c):
        p, first, num = CHUNKS[c]
        own_row = pl.multiple_of(first_row(p, core) + first, 16)
        other_row = pl.multiple_of(first_row(p, 1 - core) + first, 16)

        def put(o, _):
            for q in range(CAP):
                s = asked[o, 0, CAP * me + q]
                stage[c][o, q, :num] = left_kept[s, pl.ds(own_row, num), :]
                stage[c][o, q, num:] = left_kept[s, pl.ds(other_row, num), :]
            return 0

        lax.fori_loop(0, OWNERS - 1, put, 0)
        for o, (dx, dy) in enumerate(OFFSETS):
            pltpu.make_async_remote_copy(
                src_ref=stage[c].at[o], dst_ref=arrived[c].at[pl.ds(CAP * me, CAP)],
                send_sem=a_send.at[c], recv_sem=a_recv.at[c],
                device_id=(chan, away(SIDE - dx, SIDE - dy)), device_id_type=MESH,
            ).start()
        for q in range(CAP):
            s = asked[OWNERS - 1, 0, CAP * me + q]
            arrived[c][CAP * me + q, :num] = left_kept[s, pl.ds(own_row, num), :]
            arrived[c][CAP * me + q, num:] = left_kept[s, pl.ds(other_row, num), :]

    issue(0)
    lax.fori_loop(ASKING, ASKING + ALONE, mix, 0)
    issue(1)
    lax.fori_loop(ASKING + ALONE, ASKING + BEFORE, mix, 0)
    issue(2)

    hops = {}

    def apply_left(c, g):
        p, first, num = CHUNKS[c]

        def one(k, _):
            lhs = arrived[c][slot_smem[k]]
            for s in range(states):
                term = jnp.dot(lhs, work[k, s], preferred_element_type=F32)
                cols = slice(s * width, (s + 1) * width)
                mine[k, first : first + num, cols] = term[:num]
                give[p][k, first : first + num, cols] = term[num:].astype(BF16)
            return 0

        lax.fori_loop(g * per, (g + 1) * per, one, 0)
        part = (pl.ds(g * per, per), pl.ds(first, num))
        copy = pltpu.make_async_remote_copy(
            src_ref=give[p].at[part], dst_ref=got[p].at[part], send_sem=g_send.at[p],
            recv_sem=g_recv.at[c, g], device_id=(partner, me), device_id_type=MESH,
        )
        copy.start()
        return copy

    def combine(c, g, copy):
        p, first, num = CHUNKS[c]
        copy.wait_recv()
        for before, (q, _, _) in enumerate(CHUNKS):
            if q == p - 1:
                hops[before, g].wait_recv()
        at = slice(first, first + num)

        def one(k, _):
            total = mine[k, at] + got[p][k, at].astype(F32)
            if p:
                total = total + ring_in[p - 1][k, at].astype(F32)
            total = total.astype(BF16)
            if p < PHASES - 1:
                ring_out[p][k, at] = total
            else:
                for s in range(states):
                    out_ref[k, s, at] = total[:, s * width : (s + 1) * width]
            return 0

        lax.fori_loop(g * per, (g + 1) * per, one, 0)
        blocks_of = pl.ds(g * per, per)
        if p < PHASES - 1:
            part = (blocks_of, pl.ds(first, num))
            hops[c, g] = pltpu.make_async_remote_copy(
                src_ref=ring_out[p].at[part], dst_ref=ring_in[p].at[part],
                send_sem=n_send.at[p], recv_sem=n_recv.at[c, g],
                device_id=(up, me), device_id_type=MESH,
            )
            hops[c, g].start()

    for c in range(len(CHUNKS)):
        all_of(stage[c], a_recv.at[c]).wait()
        if c == 2:
            issue(4)
        copies = []
        for g in range(GROUPS):
            copies.append(apply_left(c, g))
            if c == 0 and g == 1:
                combine(c, 0, copies[0])
                lax.fori_loop(ASKING + BEFORE, blocks, mix, 0)
                combine(c, 1, copies[1])
            elif c == 0 and g == 2:
                issue(3)
            elif g:
                combine(c, g - 1, copies[g - 1])
        combine(c, GROUPS - 1, copies[GROUPS - 1])

    all_of(asked.at[pl.ds(0, OWNERS - 1)], tab_send).wait()
    for c in range(len(CHUNKS)):
        all_of(stage[c], a_send.at[c]).wait()
    for p in range(PHASES):
        all_of(give[p], g_send.at[p]).wait()
    for p in range(PHASES - 1):
        all_of(ring_out[p], n_send.at[p]).wait()


def on_device(psi, mpo, left_env, right_env, left_dims, right_dims, dest_owner, left_slot):
    blocks, states, width = psi.shape[0], psi.shape[1], psi.shape[2]
    sectors = left_env.shape[1]
    rows = width // (2 * Z)
    wide = states * width
    chunks = len(CHUNKS)
    smem = pl.BlockSpec(memory_space=pltpu.SMEM)
    hbm = pl.BlockSpec(memory_space=pl.ANY)
    dma = pltpu.SemaphoreType.DMA
    piece = pltpu.VMEM((blocks, rows, wide), BF16)
    return pl.pallas_call(
        kernel,
        out_shape=pltpu.VMEM((blocks, states, rows, width), BF16),
        in_specs=[smem] * 5 + [hbm] * 3,
        out_specs=pl.BlockSpec(memory_space=pltpu.VMEM),
        scratch_shapes=[
            pltpu.VMEM((sectors, width, width), BF16),
            pltpu.VMEM((1, 128), jnp.int32),
            pltpu.SMEM((OWNERS, 1, 128), jnp.int32),
            pltpu.SMEM((blocks,), jnp.int32),
            *[pltpu.VMEM((OWNERS - 1, CAP, 2 * num, width), BF16) for _, _, num in CHUNKS],
            *[pltpu.VMEM((OWNERS * CAP, 2 * num, width), BF16) for _, _, num in CHUNKS],
            pltpu.VMEM((blocks, states, width, width), BF16),
            pltpu.VMEM((blocks, width, width), BF16),
            pltpu.VMEM((blocks, rows, wide), F32),
            *[piece] * (2 * PHASES + 2 * (PHASES - 1)),
            dma,
            dma,
            dma,
            dma((chunks,)),
            dma((chunks,)),
            dma((blocks // PSI_READ,)),
            dma((blocks // RIGHT_READ,)),
            dma,
            dma((PHASES,)),
            dma((chunks, GROUPS)),
            dma((PHASES - 1,)),
            dma((chunks - 1, GROUPS)),
        ],
        compiler_params=pltpu.CompilerParams(
            collective_id=0, has_side_effects=True, vmem_limit_bytes=58 << 20
        ),
    )(mpo, left_dims, right_dims, dest_owner.reshape(blocks), left_slot, left_env, psi, right_env)


def solution(mesh):
    in_specs = (
        P("sec", None, None, None),
        P("chan", None, None),
        P("chan", "sec", None, None),
        P("chan", "sec", None, None),
        P("sec"),
        P("sec"),
        P("sec", None),
        P("sec"),
    )
    out_specs = P("sec", None, "chan", None)
    return jax.shard_map(
        on_device, mesh=mesh, in_specs=in_specs, out_specs=out_specs, check_vma=False
    )
```

```python
import functools

import jax
import jax.numpy as jnp
from jax import lax
from jax.experimental import pallas as pl
from jax.experimental.pallas import tpu as pltpu
from jax.sharding import PartitionSpec as P

MESH = pl.DeviceIdType.MESH
F32 = jnp.float32
BF16 = jnp.bfloat16

Z = 4
SIDE = 4
OWNERS = SIDE * SIDE
CAP = 2
PHASES = Z
PSI_READ = 2
RIGHT_READ = 4
ASKING = 7
ALONE = 8
BEFORE = 14
CHUNKS = ((0, 0, 16), (0, 16, 16), (1, 0, 16), (1, 16, 16), (2, 0, 32), (3, 0, 32))
EVEN = ((0, 6), (6, 6), (12, 6), (18, 6))
PIECES = (((0, 3), (3, 3), (6, 6), (12, 6), (18, 6)),) + (EVEN,) * (len(CHUNKS) - 1)
MOST = max(len(pieces) for pieces in PIECES)
OFFSETS = (
    (1, 0), (0, 1), (3, 0), (0, 3), (1, 1), (3, 3), (1, 3), (3, 1),
    (2, 0), (0, 2), (2, 1), (1, 2), (2, 3), (3, 2), (2, 2),
)


def kernel(
    mpo_hbm, left_dims_hbm, right_dims_hbm, dest_hbm, slot_hbm,
    left_hbm, psi_hbm, right_hbm, out_ref,
    mpo, left_dims, right_dims, dest, slot, left_kept, table, asked, slot_smem,
    stage0, stage1, stage2, stage3, stage4, stage5, arr0, arr1, arr2, arr3, arr4, arr5,
    work, right_all, mine, give0, give1, give2, give3, got0, got1, got2, got3,
    ring_out0, ring_out1, ring_out2, ring_in0, ring_in1, ring_in2,
    s_sem, tab_send, tab_recv, tab_local, a_send, a_recv, p_sem, r_sem, l_sem,
    g_send, g_recv, n_send, n_recv,
):
    blocks, states, width = psi_hbm.shape[0], psi_hbm.shape[1], psi_hbm.shape[2]
    sectors = left_kept.shape[0]
    rows = width // (2 * Z)
    stage = (stage0, stage1, stage2, stage3, stage4, stage5)
    arrived = (arr0, arr1, arr2, arr3, arr4, arr5)
    give = (give0, give1, give2, give3)
    got = (got0, got1, got2, got3)
    ring_out = (ring_out0, ring_out1, ring_out2)
    ring_in = (ring_in0, ring_in1, ring_in2)

    chan = lax.axis_index("chan")
    me = lax.axis_index("sec")
    z, core = chan // 2, lax.rem(chan, 2)
    y, x = me // SIDE, lax.rem(me, SIDE)
    up = lax.rem(z + 1 + 2 * core, Z) * 2 + core
    down = lax.rem(z + 3 + 2 * core, Z) * 2 + core
    partner = z * 2 + 1 - core

    def away(dx, dy):
        return lax.rem(y + dy, SIDE) * SIDE + lax.rem(x + dx, SIDE)

    barrier = pltpu.get_barrier_semaphore()
    for dx, dy in OFFSETS[::-1]:
        pl.semaphore_signal(barrier, inc=1, device_id=(chan, away(dx, dy)), device_id_type=MESH)
    for other in (down, partner):
        pl.semaphore_signal(barrier, inc=1, device_id=(other, me), device_id_type=MESH)

    small = [
        pltpu.make_async_copy(source, target, s_sem.at[i])
        for i, (source, target) in enumerate(
            ((dest_hbm, dest), (slot_hbm, slot), (right_dims_hbm, right_dims),
             (left_dims_hbm, left_dims), (mpo_hbm, mpo))
        )
    ]
    for copy in small:
        copy.start()

    def psi_copy(i):
        part = pl.ds(i * PSI_READ, PSI_READ)
        return pltpu.make_async_copy(psi_hbm.at[part], work.at[part], p_sem.at[i])

    def right_copy(i):
        part = pl.ds(i * RIGHT_READ, RIGHT_READ)
        return pltpu.make_async_copy(right_hbm.at[0, part], right_all.at[part], r_sem.at[i])

    def all_of(ref, sem):
        return pltpu.make_async_copy(ref, ref, sem)

    left_copy = pltpu.make_async_copy(left_hbm.at[0], left_kept, l_sem)

    def read(first, last):
        for k in range(first, last):
            if k % RIGHT_READ == 0:
                right_copy(k // RIGHT_READ).start()
            if k % PSI_READ == 0:
                psi_copy(k // PSI_READ).start()

    read(0, ASKING)
    left_copy.start()

    lane = lax.broadcasted_iota(jnp.int32, (1, 128), 1)
    lane_owner, lane_place = lane // CAP, lax.rem(lane, CAP)
    small[0].wait()
    small[1].wait()
    wanted = jnp.zeros((1, 128), jnp.int32)
    count = jnp.zeros((1, 128), jnp.int32)
    for k in range(blocks):
        own = lane_owner == dest[k]
        wanted = jnp.where(own & (count == lane_place), slot[k], wanted)
        count = count + jnp.where(own, 1, 0)
    table[...] = wanted

    pl.semaphore_wait(barrier, len(OFFSETS) + 2)

    for o, (dx, dy) in list(enumerate(OFFSETS))[::-1]:
        pltpu.make_async_remote_copy(
            src_ref=table, dst_ref=asked.at[o], send_sem=tab_send, recv_sem=tab_recv,
            device_id=(chan, away(dx, dy)), device_id_type=MESH,
        ).start()
    own_ask = pltpu.make_async_copy(table, asked.at[OWNERS - 1], tab_local)
    own_ask.start()
    read(ASKING, blocks)

    row_at = lax.broadcasted_iota(jnp.int32, (width, width), 0)
    col_at = lax.broadcasted_iota(jnp.int32, (width, width), 1)

    def kept(values, dim):
        mask = jnp.where((row_at < dim) & (col_at < dim), 1.0, 0.0).astype(BF16)
        return values * mask

    def mix(k, _):
        @pl.when(lax.rem(k, RIGHT_READ) == 0)
        def _():
            right_copy(k // RIGHT_READ).wait()

        @pl.when(lax.rem(k, PSI_READ) == 0)
        def _():
            psi_copy(k // PSI_READ).wait()

        right = kept(right_all[k], right_dims[k])
        inner = lax.dot_general(
            work[k].reshape(states * width, width), right, (((1,), (1,)), ((), ())),
            preferred_element_type=F32,
        )
        for s in range(states):
            total = mpo[0, s, 0] * inner[:width]
            for p in range(1, states):
                total = total + mpo[0, s, p] * inner[p * width : (p + 1) * width]
            work[k, s] = total.astype(BF16)
        return 0

    def keep_left(s, _):
        left_kept[s] = kept(left_kept[s], left_dims[s])
        return 0

    for copy in small[2:]:
        copy.wait()
    lax.fori_loop(0, ASKING, mix, 0)
    left_copy.wait()
    lax.fori_loop(0, sectors, keep_left, 0)

    all_of(asked.at[pl.ds(0, OWNERS - 1)], tab_recv).wait()

    own_ask.wait()

    def first_row(p, c):
        chip = jnp.where(c == 0, lax.rem(z + 3 - p + Z, Z), lax.rem(z + 1 + p, Z))
        return (chip * 2 + c) * rows

    def issue(c):
        p, first, num = CHUNKS[c]
        own_row = pl.multiple_of(first_row(p, core) + first, 16)
        other_row = pl.multiple_of(first_row(p, 1 - core) + first, 16)

        def put(o, _):
            for q in range(CAP):
                s = asked[o, 0, CAP * me + q]
                stage[c][o, q, :num] = left_kept[s, pl.ds(own_row, num), :]
                stage[c][o, q, num:] = left_kept[s, pl.ds(other_row, num), :]
            return 0

        lax.fori_loop(0, OWNERS - 1, put, 0)
        for o, (dx, dy) in enumerate(OFFSETS):
            pltpu.make_async_remote_copy(
                src_ref=stage[c].at[o], dst_ref=arrived[c].at[pl.ds(CAP * me, CAP)],
                send_sem=a_send.at[c], recv_sem=a_recv.at[c],
                device_id=(chan, away(SIDE - dx, SIDE - dy)), device_id_type=MESH,
            ).start()
        for q in range(CAP):
            s = asked[OWNERS - 1, 0, CAP * me + q]
            arrived[c][CAP * me + q, :num] = left_kept[s, pl.ds(own_row, num), :]
            arrived[c][CAP * me + q, num:] = left_kept[s, pl.ds(other_row, num), :]

    issue(0)
    for k in range(blocks):
        place = dest[k] * CAP
        for before in range(k):
            place = place + jnp.where(dest[before] == dest[k], 1, 0)
        slot_smem[k] = place

    lax.fori_loop(ASKING, ASKING + ALONE, mix, 0)
    issue(1)
    lax.fori_loop(ASKING + ALONE, ASKING + BEFORE, mix, 0)
    issue(2)

    hops = {}

    def apply_left(c, g):
        p, first, num = CHUNKS[c]
        start, size = PIECES[c][g]

        def one(k, _):
            lhs = arrived[c][slot_smem[k]]
            for s in range(states):
                term = jnp.dot(lhs, work[k, s], preferred_element_type=F32)
                cols = slice(s * width, (s + 1) * width)
                mine[k, first : first + num, cols] = term[:num]
                give[p][k, first : first + num, cols] = term[num:].astype(BF16)
            return 0

        lax.fori_loop(start, start + size, one, 0)
        part = (pl.ds(start, size), pl.ds(first, num))
        copy = pltpu.make_async_remote_copy(
            src_ref=give[p].at[part], dst_ref=got[p].at[part], send_sem=g_send.at[p],
            recv_sem=g_recv.at[c, g], device_id=(partner, me), device_id_type=MESH,
        )
        copy.start()
        return copy

    def combine(c, g, copy):
        p, first, num = CHUNKS[c]
        start, size = PIECES[c][g]
        copy.wait_recv()
        for before, (q, row, many) in enumerate(CHUNKS):
            for i, (block, count) in enumerate(PIECES[before]):
                here = block < start + size and start < block + count
                if q == p - 1 and row < first + num and first < row + many and here:
                    if (before, i) in hops:
                        hops.pop((before, i)).wait_recv()
        at = slice(first, first + num)

        def one(k, _):
            total = mine[k, at] + got[p][k, at].astype(F32)
            if p:
                total = total + ring_in[p - 1][k, at].astype(F32)
            total = total.astype(BF16)
            if p < PHASES - 1:
                ring_out[p][k, at] = total
            else:
                for s in range(states):
                    out_ref[k, s, at] = total[:, s * width : (s + 1) * width]
            return 0

        lax.fori_loop(start, start + size, one, 0)
        if p < PHASES - 1:
            part = (pl.ds(start, size), pl.ds(first, num))
            hops[c, g] = pltpu.make_async_remote_copy(
                src_ref=ring_out[p].at[part], dst_ref=ring_in[p].at[part],
                send_sem=n_send.at[p], recv_sem=n_recv.at[c, g],
                device_id=(up, me), device_id_type=MESH,
            )
            hops[c, g].start()

    for c in range(len(CHUNKS)):
        all_of(stage[c], a_recv.at[c]).wait()
        if c in (2, 3):
            issue(c + 2)
        copies = []
        if c == 0:
            copies = [apply_left(c, g) for g in range(3)]
            combine(c, 0, copies[0])
            combine(c, 1, copies[1])
            lax.fori_loop(ASKING + BEFORE, blocks, mix, 0)
            combine(c, 2, copies[2])
            copies += [apply_left(c, g) for g in (3, 4)]
            combine(c, 3, copies[3])
            combine(c, 4, copies[4])
            issue(3)
        else:
            for g in range(len(PIECES[c])):
                copies.append(apply_left(c, g))
                if g:
                    combine(c, g - 1, copies[g - 1])
            combine(c, len(PIECES[c]) - 1, copies[-1])

    all_of(asked.at[pl.ds(0, OWNERS - 1)], tab_send).wait()
    for c in range(len(CHUNKS)):
        all_of(stage[c], a_send.at[c]).wait()
    for p in range(PHASES):
        all_of(give[p], g_send.at[p]).wait()
    for p in range(PHASES - 1):
        all_of(ring_out[p], n_send.at[p]).wait()


def on_device(psi, mpo, left_env, right_env, left_dims, right_dims, dest_owner, left_slot):
    blocks, states, width = psi.shape[0], psi.shape[1], psi.shape[2]
    sectors = left_env.shape[1]
    rows = width // (2 * Z)
    wide = states * width
    chunks = len(CHUNKS)
    hbm = pl.BlockSpec(memory_space=pl.ANY)
    dma = pltpu.SemaphoreType.DMA
    piece = pltpu.VMEM((blocks, rows, wide), BF16)
    return pl.pallas_call(
        kernel,
        out_shape=pltpu.VMEM((blocks, states, rows, width), BF16),
        in_specs=[hbm] * 8,
        out_specs=pl.BlockSpec(memory_space=pltpu.VMEM),
        scratch_shapes=[
            pltpu.SMEM(mpo.shape, F32),
            pltpu.SMEM((sectors,), jnp.int32),
            pltpu.SMEM((blocks,), jnp.int32),
            pltpu.SMEM((blocks,), jnp.int32),
            pltpu.SMEM((blocks,), jnp.int32),
            pltpu.VMEM((sectors, width, width), BF16),
            pltpu.VMEM((1, 128), jnp.int32),
            pltpu.SMEM((OWNERS, 1, 128), jnp.int32),
            pltpu.SMEM((blocks,), jnp.int32),
            *[pltpu.VMEM((OWNERS - 1, CAP, 2 * num, width), BF16) for _, _, num in CHUNKS],
            *[pltpu.VMEM((OWNERS * CAP, 2 * num, width), BF16) for _, _, num in CHUNKS],
            pltpu.VMEM((blocks, states, width, width), BF16),
            pltpu.VMEM((blocks, width, width), BF16),
            pltpu.VMEM((blocks, rows, wide), F32),
            *[piece] * (2 * PHASES + 2 * (PHASES - 1)),
            dma((5,)),
            dma,
            dma,
            dma,
            dma((chunks,)),
            dma((chunks,)),
            dma((blocks // PSI_READ,)),
            dma((blocks // RIGHT_READ,)),
            dma,
            dma((PHASES,)),
            dma((chunks, MOST)),
            dma((PHASES - 1,)),
            dma((chunks - 1, MOST)),
        ],
        compiler_params=pltpu.CompilerParams(
            collective_id=0, has_side_effects=True, vmem_limit_bytes=58 << 20
        ),
    )(mpo, left_dims, right_dims, dest_owner.reshape(blocks), left_slot, left_env, psi, right_env)


def solution(mesh):
    in_specs = (
        P("sec", None, None, None),
        P("chan", None, None),
        P("chan", "sec", None, None),
        P("chan", "sec", None, None),
        P("sec"),
        P("sec"),
        P("sec", None),
        P("sec"),
    )
    out_specs = P("sec", None, "chan", None)
    return jax.shard_map(
        on_device, mesh=mesh, in_specs=in_specs, out_specs=out_specs, check_vma=False
    )
```

```python
import functools

import jax
import jax.numpy as jnp
from jax import lax
from jax.experimental import pallas as pl
from jax.experimental.pallas import tpu as pltpu
from jax.sharding import PartitionSpec as P

MESH = pl.DeviceIdType.MESH
F32 = jnp.float32
BF16 = jnp.bfloat16

Z = 4
SIDE = 4
OWNERS = SIDE * SIDE
CAP = 2
PHASES = Z
PSI_READ = 2
RIGHT_READ = 4
ASKING = 7
ALONE = 10
BEFORE = 14
CHUNKS = ((0, 0, 16), (0, 16, 16), (1, 0, 16), (1, 16, 16), (2, 0, 32), (3, 0, 32))
EVEN = ((0, 6), (6, 6), (12, 6), (18, 6))
PIECES = (((0, 3), (3, 3), (6, 6), (12, 6), (18, 6)),) + (EVEN,) * (len(CHUNKS) - 1)
MOST = max(len(pieces) for pieces in PIECES)
OFFSETS = (
    (1, 0), (0, 1), (3, 0), (0, 3), (2, 1), (1, 2), (2, 3), (3, 2), (1, 1), (3, 3), (1, 3), (3, 1), (2, 0), (0, 2), (2, 2),
)


def kernel(
    mpo_hbm, left_dims_hbm, right_dims_hbm, dest_hbm, slot_hbm,
    left_hbm, psi_hbm, right_hbm, out_ref,
    mpo, left_dims, right_dims, dest, slot, left_kept, table, asked, slot_smem,
    stage0, stage1, stage2, stage3, stage4, stage5, arr0, arr1, arr2, arr3, arr4, arr5,
    work, right_all, mine, give0, give1, give2, give3, got0, got1, got2, got3,
    ring_out0, ring_out1, ring_out2, ring_in0, ring_in1, ring_in2,
    s_sem, tab_send, tab_recv, tab_local, a_send, a_recv, p_sem, r_sem, l_sem,
    g_send, g_recv, n_send, n_recv,
):
    blocks, states, width = psi_hbm.shape[0], psi_hbm.shape[1], psi_hbm.shape[2]
    sectors = left_kept.shape[0]
    rows = width // (2 * Z)
    stage = (stage0, stage1, stage2, stage3, stage4, stage5)
    arrived = (arr0, arr1, arr2, arr3, arr4, arr5)
    give = (give0, give1, give2, give3)
    got = (got0, got1, got2, got3)
    ring_out = (ring_out0, ring_out1, ring_out2)
    ring_in = (ring_in0, ring_in1, ring_in2)

    chan = lax.axis_index("chan")
    me = lax.axis_index("sec")
    z, core = chan // 2, lax.rem(chan, 2)
    y, x = me // SIDE, lax.rem(me, SIDE)
    up = lax.rem(z + 1 + 2 * core, Z) * 2 + core
    down = lax.rem(z + 3 + 2 * core, Z) * 2 + core
    partner = z * 2 + 1 - core

    def away(dx, dy):
        return lax.rem(y + dy, SIDE) * SIDE + lax.rem(x + dx, SIDE)

    barrier = pltpu.get_barrier_semaphore()
    for dx, dy in OFFSETS[::-1]:
        pl.semaphore_signal(barrier, inc=1, device_id=(chan, away(dx, dy)), device_id_type=MESH)
    for other in (down, partner):
        pl.semaphore_signal(barrier, inc=1, device_id=(other, me), device_id_type=MESH)

    small = [
        pltpu.make_async_copy(source, target, s_sem.at[i])
        for i, (source, target) in enumerate(
            ((dest_hbm, dest), (slot_hbm, slot), (right_dims_hbm, right_dims),
             (left_dims_hbm, left_dims), (mpo_hbm, mpo))
        )
    ]
    for copy in small:
        copy.start()

    def psi_copy(i):
        part = pl.ds(i * PSI_READ, PSI_READ)
        return pltpu.make_async_copy(psi_hbm.at[part], work.at[part], p_sem.at[i])

    def right_copy(i):
        part = pl.ds(i * RIGHT_READ, RIGHT_READ)
        return pltpu.make_async_copy(right_hbm.at[0, part], right_all.at[part], r_sem.at[i])

    def all_of(ref, sem):
        return pltpu.make_async_copy(ref, ref, sem)

    left_copy = pltpu.make_async_copy(left_hbm.at[0], left_kept, l_sem)

    def read(first, last):
        for k in range(first, last):
            if k % RIGHT_READ == 0:
                right_copy(k // RIGHT_READ).start()
            if k % PSI_READ == 0:
                psi_copy(k // PSI_READ).start()

    read(0, ASKING)
    left_copy.start()

    lane = lax.broadcasted_iota(jnp.int32, (1, 128), 1)
    lane_owner, lane_place = lane // CAP, lax.rem(lane, CAP)
    small[0].wait()
    small[1].wait()
    wanted = jnp.zeros((1, 128), jnp.int32)
    count = jnp.zeros((1, 128), jnp.int32)
    for k in range(blocks):
        own = lane_owner == dest[k]
        wanted = jnp.where(own & (count == lane_place), slot[k], wanted)
        count = count + jnp.where(own, 1, 0)
    table[...] = wanted

    pl.semaphore_wait(barrier, len(OFFSETS) + 2)

    for o, (dx, dy) in list(enumerate(OFFSETS))[::-1]:
        pltpu.make_async_remote_copy(
            src_ref=table, dst_ref=asked.at[o], send_sem=tab_send, recv_sem=tab_recv,
            device_id=(chan, away(dx, dy)), device_id_type=MESH,
        ).start()
    own_ask = pltpu.make_async_copy(table, asked.at[OWNERS - 1], tab_local)
    own_ask.start()
    read(ASKING, blocks)

    row_at = lax.broadcasted_iota(jnp.int32, (width, width), 0)
    col_at = lax.broadcasted_iota(jnp.int32, (width, width), 1)

    def kept(values, dim):
        mask = jnp.where((row_at < dim) & (col_at < dim), 1.0, 0.0).astype(BF16)
        return values * mask

    def mix(k, _):
        @pl.when(lax.rem(k, RIGHT_READ) == 0)
        def _():
            right_copy(k // RIGHT_READ).wait()

        @pl.when(lax.rem(k, PSI_READ) == 0)
        def _():
            psi_copy(k // PSI_READ).wait()

        right = kept(right_all[k], right_dims[k])
        inner = lax.dot_general(
            work[k].reshape(states * width, width), right, (((1,), (1,)), ((), ())),
            preferred_element_type=F32,
        )
        for s in range(states):
            total = mpo[0, s, 0] * inner[:width]
            for p in range(1, states):
                total = total + mpo[0, s, p] * inner[p * width : (p + 1) * width]
            work[k, s] = total.astype(BF16)
        return 0

    def keep_left(s, _):
        left_kept[s] = kept(left_kept[s], left_dims[s])
        return 0

    for copy in small[2:]:
        copy.wait()
    lax.fori_loop(0, ASKING, mix, 0)
    left_copy.wait()
    lax.fori_loop(0, sectors, keep_left, 0)

    all_of(asked.at[pl.ds(0, OWNERS - 1)], tab_recv).wait()

    own_ask.wait()

    def first_row(p, c):
        chip = jnp.where(c == 0, lax.rem(z + 3 - p + Z, Z), lax.rem(z + 1 + p, Z))
        return (chip * 2 + c) * rows

    def issue(c):
        p, first, num = CHUNKS[c]
        own_row = pl.multiple_of(first_row(p, core) + first, 16)
        other_row = pl.multiple_of(first_row(p, 1 - core) + first, 16)

        def put(o, _):
            for q in range(CAP):
                s = asked[o, 0, CAP * me + q]
                stage[c][o, q, :num] = left_kept[s, pl.ds(own_row, num), :]
                stage[c][o, q, num:] = left_kept[s, pl.ds(other_row, num), :]
            return 0

        lax.fori_loop(0, OWNERS - 1, put, 0)
        for o, (dx, dy) in enumerate(OFFSETS):
            pltpu.make_async_remote_copy(
                src_ref=stage[c].at[o], dst_ref=arrived[c].at[pl.ds(CAP * me, CAP)],
                send_sem=a_send.at[c], recv_sem=a_recv.at[c],
                device_id=(chan, away(SIDE - dx, SIDE - dy)), device_id_type=MESH,
            ).start()
        for q in range(CAP):
            s = asked[OWNERS - 1, 0, CAP * me + q]
            arrived[c][CAP * me + q, :num] = left_kept[s, pl.ds(own_row, num), :]
            arrived[c][CAP * me + q, num:] = left_kept[s, pl.ds(other_row, num), :]

    issue(0)
    for k in range(blocks):
        place = dest[k] * CAP
        for before in range(k):
            place = place + jnp.where(dest[before] == dest[k], 1, 0)
        slot_smem[k] = place

    lax.fori_loop(ASKING, ASKING + ALONE, mix, 0)
    issue(1)
    lax.fori_loop(ASKING + ALONE, ASKING + BEFORE, mix, 0)
    issue(2)

    hops = {}

    def apply_left(c, g):
        p, first, num = CHUNKS[c]
        start, size = PIECES[c][g]

        def one(k, _):
            lhs = arrived[c][slot_smem[k]]
            for s in range(states):
                term = jnp.dot(lhs, work[k, s], preferred_element_type=F32)
                cols = slice(s * width, (s + 1) * width)
                mine[k, first : first + num, cols] = term[:num]
                give[p][k, first : first + num, cols] = term[num:].astype(BF16)
            return 0

        lax.fori_loop(start, start + size, one, 0)
        part = (pl.ds(start, size), pl.ds(first, num))
        copy = pltpu.make_async_remote_copy(
            src_ref=give[p].at[part], dst_ref=got[p].at[part], send_sem=g_send.at[p],
            recv_sem=g_recv.at[c, g], device_id=(partner, me), device_id_type=MESH,
        )
        copy.start()
        return copy

    def combine(c, g, copy):
        p, first, num = CHUNKS[c]
        start, size = PIECES[c][g]
        copy.wait_recv()
        for before, (q, row, many) in enumerate(CHUNKS):
            for i, (block, count) in enumerate(PIECES[before]):
                here = block < start + size and start < block + count
                if q == p - 1 and row < first + num and first < row + many and here:
                    if (before, i) in hops:
                        hops.pop((before, i)).wait_recv()
        at = slice(first, first + num)

        def one(k, _):
            total = mine[k, at] + got[p][k, at].astype(F32)
            if p:
                total = total + ring_in[p - 1][k, at].astype(F32)
            total = total.astype(BF16)
            if p < PHASES - 1:
                ring_out[p][k, at] = total
            else:
                for s in range(states):
                    out_ref[k, s, at] = total[:, s * width : (s + 1) * width]
            return 0

        lax.fori_loop(start, start + size, one, 0)
        if p < PHASES - 1:
            part = (pl.ds(start, size), pl.ds(first, num))
            hops[c, g] = pltpu.make_async_remote_copy(
                src_ref=ring_out[p].at[part], dst_ref=ring_in[p].at[part],
                send_sem=n_send.at[p], recv_sem=n_recv.at[c, g],
                device_id=(up, me), device_id_type=MESH,
            )
            hops[c, g].start()

    for c in range(len(CHUNKS)):
        all_of(stage[c], a_recv.at[c]).wait()
        if c in (2, 3):
            issue(c + 2)
        copies = []
        if c == 0:
            copies = [apply_left(c, g) for g in range(3)]
            combine(c, 0, copies[0])
            combine(c, 1, copies[1])
            lax.fori_loop(ASKING + BEFORE, blocks, mix, 0)
            combine(c, 2, copies[2])
            copies += [apply_left(c, g) for g in (3, 4)]
            combine(c, 3, copies[3])
            combine(c, 4, copies[4])
            issue(3)
        else:
            for g in range(len(PIECES[c])):
                copies.append(apply_left(c, g))
                if g:
                    combine(c, g - 1, copies[g - 1])
            combine(c, len(PIECES[c]) - 1, copies[-1])

    all_of(asked.at[pl.ds(0, OWNERS - 1)], tab_send).wait()
    for c in range(len(CHUNKS)):
        all_of(stage[c], a_send.at[c]).wait()
    for p in range(PHASES):
        all_of(give[p], g_send.at[p]).wait()
    for p in range(PHASES - 1):
        all_of(ring_out[p], n_send.at[p]).wait()


def on_device(psi, mpo, left_env, right_env, left_dims, right_dims, dest_owner, left_slot):
    blocks, states, width = psi.shape[0], psi.shape[1], psi.shape[2]
    sectors = left_env.shape[1]
    rows = width // (2 * Z)
    wide = states * width
    chunks = len(CHUNKS)
    hbm = pl.BlockSpec(memory_space=pl.ANY)
    dma = pltpu.SemaphoreType.DMA
    piece = pltpu.VMEM((blocks, rows, wide), BF16)
    return pl.pallas_call(
        kernel,
        out_shape=pltpu.VMEM((blocks, states, rows, width), BF16),
        in_specs=[hbm] * 8,
        out_specs=pl.BlockSpec(memory_space=pltpu.VMEM),
        scratch_shapes=[
            pltpu.SMEM(mpo.shape, F32),
            pltpu.SMEM((sectors,), jnp.int32),
            pltpu.SMEM((blocks,), jnp.int32),
            pltpu.SMEM((blocks,), jnp.int32),
            pltpu.SMEM((blocks,), jnp.int32),
            pltpu.VMEM((sectors, width, width), BF16),
            pltpu.VMEM((1, 128), jnp.int32),
            pltpu.SMEM((OWNERS, 1, 128), jnp.int32),
            pltpu.SMEM((blocks,), jnp.int32),
            *[pltpu.VMEM((OWNERS - 1, CAP, 2 * num, width), BF16) for _, _, num in CHUNKS],
            *[pltpu.VMEM((OWNERS * CAP, 2 * num, width), BF16) for _, _, num in CHUNKS],
            pltpu.VMEM((blocks, states, width, width), BF16),
            pltpu.VMEM((blocks, width, width), BF16),
            pltpu.VMEM((blocks, rows, wide), F32),
            *[piece] * (2 * PHASES + 2 * (PHASES - 1)),
            dma((5,)),
            dma,
            dma,
            dma,
            dma((chunks,)),
            dma((chunks,)),
            dma((blocks // PSI_READ,)),
            dma((blocks // RIGHT_READ,)),
            dma,
            dma((PHASES,)),
            dma((chunks, MOST)),
            dma((PHASES - 1,)),
            dma((chunks - 1, MOST)),
        ],
        compiler_params=pltpu.CompilerParams(
            collective_id=0, has_side_effects=True, vmem_limit_bytes=58 << 20
        ),
    )(mpo, left_dims, right_dims, dest_owner.reshape(blocks), left_slot, left_env, psi, right_env)


def solution(mesh):
    in_specs = (
        P("sec", None, None, None),
        P("chan", None, None),
        P("chan", "sec", None, None),
        P("chan", "sec", None, None),
        P("sec"),
        P("sec"),
        P("sec", None),
        P("sec"),
    )
    out_specs = P("sec", None, "chan", None)
    return jax.shard_map(
        on_device, mesh=mesh, in_specs=in_specs, out_specs=out_specs, check_vma=False
    )
```

```python
import functools

import jax
import jax.numpy as jnp
from jax import lax
from jax.experimental import pallas as pl
from jax.experimental.pallas import tpu as pltpu
from jax.sharding import PartitionSpec as P

MESH = pl.DeviceIdType.MESH
F32 = jnp.float32
BF16 = jnp.bfloat16

Z = 4
SIDE = 4
OWNERS = SIDE * SIDE
CAP = 2
PHASES = Z
PSI_READ = 4
RIGHT_READ = 4
ASKING = 7
ALONE = 10
BEFORE = 14
CHUNKS = ((0, 0, 16), (0, 16, 16), (1, 0, 16), (1, 16, 16), (2, 0, 32), (3, 0, 32))
EVEN = ((0, 6), (6, 6), (12, 6), (18, 6))
PIECES = (((0, 3), (3, 3), (6, 6), (12, 6), (18, 6)),) + (EVEN,) * (len(CHUNKS) - 1)
MOST = max(len(pieces) for pieces in PIECES)
OFFSETS = (
    (1, 0), (0, 1), (3, 0), (0, 3), (2, 1), (1, 2), (2, 3), (3, 2), (1, 1), (3, 3), (1, 3), (3, 1), (2, 0), (0, 2), (2, 2),
)


def kernel(
    mpo_hbm, left_dims_hbm, right_dims_hbm, dest_hbm, slot_hbm,
    left_hbm, psi_hbm, right_hbm, out_ref,
    mpo, left_dims, right_dims, dest, slot, left_kept, table, asked, slot_smem,
    stage0, stage1, stage2, stage3, stage4, stage5, arr0, arr1, arr2, arr3, arr4, arr5,
    work, right_all, mine, give0, give1, give2, give3, got0, got1, got2, got3,
    ring_out0, ring_out1, ring_out2, ring_in0, ring_in1, ring_in2,
    s_sem, tab_send, tab_recv, tab_local, a_send, a_recv, p_sem, r_sem, l_sem,
    g_send, g_recv, n_send, n_recv,
):
    blocks, states, width = psi_hbm.shape[0], psi_hbm.shape[1], psi_hbm.shape[2]
    sectors = left_kept.shape[0]
    rows = width // (2 * Z)
    stage = (stage0, stage1, stage2, stage3, stage4, stage5)
    arrived = (arr0, arr1, arr2, arr3, arr4, arr5)
    give = (give0, give1, give2, give3)
    got = (got0, got1, got2, got3)
    ring_out = (ring_out0, ring_out1, ring_out2)
    ring_in = (ring_in0, ring_in1, ring_in2)

    chan = lax.axis_index("chan")
    me = lax.axis_index("sec")
    z, core = chan // 2, lax.rem(chan, 2)
    y, x = me // SIDE, lax.rem(me, SIDE)
    up = lax.rem(z + 1 + 2 * core, Z) * 2 + core
    down = lax.rem(z + 3 + 2 * core, Z) * 2 + core
    partner = z * 2 + 1 - core

    def away(dx, dy):
        return lax.rem(y + dy, SIDE) * SIDE + lax.rem(x + dx, SIDE)

    barrier = pltpu.get_barrier_semaphore()
    for dx, dy in OFFSETS[::-1]:
        pl.semaphore_signal(barrier, inc=1, device_id=(chan, away(dx, dy)), device_id_type=MESH)
    for other in (down, partner):
        pl.semaphore_signal(barrier, inc=1, device_id=(other, me), device_id_type=MESH)

    small = [
        pltpu.make_async_copy(source, target, s_sem.at[i])
        for i, (source, target) in enumerate(
            ((dest_hbm, dest), (slot_hbm, slot), (right_dims_hbm, right_dims),
             (left_dims_hbm, left_dims), (mpo_hbm, mpo))
        )
    ]
    for copy in small:
        copy.start()

    def psi_copy(i):
        part = pl.ds(i * PSI_READ, PSI_READ)
        return pltpu.make_async_copy(psi_hbm.at[part], work.at[part], p_sem.at[i])

    def right_copy(i):
        part = pl.ds(i * RIGHT_READ, RIGHT_READ)
        return pltpu.make_async_copy(right_hbm.at[0, part], right_all.at[part], r_sem.at[i])

    def all_of(ref, sem):
        return pltpu.make_async_copy(ref, ref, sem)

    left_copy = pltpu.make_async_copy(left_hbm.at[0], left_kept, l_sem)

    def read(first, last):
        for k in range(first, last):
            if k % RIGHT_READ == 0:
                right_copy(k // RIGHT_READ).start()
            if k % PSI_READ == 0:
                psi_copy(k // PSI_READ).start()

    read(0, ASKING)
    left_copy.start()

    lane = lax.broadcasted_iota(jnp.int32, (1, 128), 1)
    lane_owner, lane_place = lane // CAP, lax.rem(lane, CAP)
    small[0].wait()
    small[1].wait()
    wanted = jnp.zeros((1, 128), jnp.int32)
    count = jnp.zeros((1, 128), jnp.int32)
    for k in range(blocks):
        own = lane_owner == dest[k]
        wanted = jnp.where(own & (count == lane_place), slot[k], wanted)
        count = count + jnp.where(own, 1, 0)
    table[...] = wanted

    pl.semaphore_wait(barrier, len(OFFSETS) + 2)

    for o, (dx, dy) in list(enumerate(OFFSETS))[::-1]:
        pltpu.make_async_remote_copy(
            src_ref=table, dst_ref=asked.at[o], send_sem=tab_send, recv_sem=tab_recv,
            device_id=(chan, away(dx, dy)), device_id_type=MESH,
        ).start()
    own_ask = pltpu.make_async_copy(table, asked.at[OWNERS - 1], tab_local)
    own_ask.start()
    read(ASKING, blocks)

    row_at = lax.broadcasted_iota(jnp.int32, (width, width), 0)
    col_at = lax.broadcasted_iota(jnp.int32, (width, width), 1)

    def kept(values, dim):
        mask = jnp.where((row_at < dim) & (col_at < dim), 1.0, 0.0).astype(BF16)
        return values * mask

    def mix(k, _):
        @pl.when(lax.rem(k, RIGHT_READ) == 0)
        def _():
            right_copy(k // RIGHT_READ).wait()

        @pl.when(lax.rem(k, PSI_READ) == 0)
        def _():
            psi_copy(k // PSI_READ).wait()

        right = kept(right_all[k], right_dims[k])
        inner = lax.dot_general(
            work[k].reshape(states * width, width), right, (((1,), (1,)), ((), ())),
            preferred_element_type=F32,
        )
        for s in range(states):
            total = mpo[0, s, 0] * inner[:width]
            for p in range(1, states):
                total = total + mpo[0, s, p] * inner[p * width : (p + 1) * width]
            work[k, s] = total.astype(BF16)
        return 0

    def keep_left(s, _):
        left_kept[s] = kept(left_kept[s], left_dims[s])
        return 0

    for copy in small[2:]:
        copy.wait()
    lax.fori_loop(0, ASKING, mix, 0)
    left_copy.wait()
    lax.fori_loop(0, sectors, keep_left, 0)

    all_of(asked.at[pl.ds(0, OWNERS - 1)], tab_recv).wait()

    own_ask.wait()

    def first_row(p, c):
        chip = jnp.where(c == 0, lax.rem(z + 3 - p + Z, Z), lax.rem(z + 1 + p, Z))
        return (chip * 2 + c) * rows

    def issue(c):
        p, first, num = CHUNKS[c]
        own_row = pl.multiple_of(first_row(p, core) + first, 16)
        other_row = pl.multiple_of(first_row(p, 1 - core) + first, 16)

        def put(o, _):
            for q in range(CAP):
                s = asked[o, 0, CAP * me + q]
                stage[c][o, q, :num] = left_kept[s, pl.ds(own_row, num), :]
                stage[c][o, q, num:] = left_kept[s, pl.ds(other_row, num), :]
            return 0

        lax.fori_loop(0, OWNERS - 1, put, 0)
        for o, (dx, dy) in enumerate(OFFSETS):
            pltpu.make_async_remote_copy(
                src_ref=stage[c].at[o], dst_ref=arrived[c].at[pl.ds(CAP * me, CAP)],
                send_sem=a_send.at[c], recv_sem=a_recv.at[c],
                device_id=(chan, away(SIDE - dx, SIDE - dy)), device_id_type=MESH,
            ).start()
        for q in range(CAP):
            s = asked[OWNERS - 1, 0, CAP * me + q]
            arrived[c][CAP * me + q, :num] = left_kept[s, pl.ds(own_row, num), :]
            arrived[c][CAP * me + q, num:] = left_kept[s, pl.ds(other_row, num), :]

    issue(0)
    for k in range(blocks):
        place = dest[k] * CAP
        for before in range(k):
            place = place + jnp.where(dest[before] == dest[k], 1, 0)
        slot_smem[k] = place

    lax.fori_loop(ASKING, ASKING + ALONE, mix, 0)
    issue(1)
    lax.fori_loop(ASKING + ALONE, ASKING + BEFORE, mix, 0)
    issue(2)

    hops = {}

    def apply_left(c, g):
        p, first, num = CHUNKS[c]
        start, size = PIECES[c][g]

        def one(k, _):
            lhs = arrived[c][slot_smem[k]]
            for s in range(states):
                term = jnp.dot(lhs, work[k, s], preferred_element_type=F32)
                cols = slice(s * width, (s + 1) * width)
                mine[k, first : first + num, cols] = term[:num]
                give[p][k, first : first + num, cols] = term[num:].astype(BF16)
            return 0

        lax.fori_loop(start, start + size, one, 0)
        part = (pl.ds(start, size), pl.ds(first, num))
        copy = pltpu.make_async_remote_copy(
            src_ref=give[p].at[part], dst_ref=got[p].at[part], send_sem=g_send.at[p],
            recv_sem=g_recv.at[c % 2, g], device_id=(partner, me), device_id_type=MESH,
        )
        copy.start()
        return copy

    def combine(c, g, copy):
        p, first, num = CHUNKS[c]
        start, size = PIECES[c][g]
        copy.wait_recv()
        for before, (q, row, many) in enumerate(CHUNKS):
            for i, (block, count) in enumerate(PIECES[before]):
                here = block < start + size and start < block + count
                if q == p - 1 and row < first + num and first < row + many and here:
                    if (before, i) in hops:
                        hops.pop((before, i)).wait_recv()
        at = slice(first, first + num)

        def one(k, _):
            total = mine[k, at] + got[p][k, at].astype(F32)
            if p:
                total = total + ring_in[p - 1][k, at].astype(F32)
            total = total.astype(BF16)
            if p < PHASES - 1:
                ring_out[p][k, at] = total
            else:
                for s in range(states):
                    out_ref[k, s, at] = total[:, s * width : (s + 1) * width]
            return 0

        lax.fori_loop(start, start + size, one, 0)
        if p < PHASES - 1:
            part = (pl.ds(start, size), pl.ds(first, num))
            hops[c, g] = pltpu.make_async_remote_copy(
                src_ref=ring_out[p].at[part], dst_ref=ring_in[p].at[part],
                send_sem=n_send.at[p], recv_sem=n_recv.at[c, g],
                device_id=(up, me), device_id_type=MESH,
            )
            hops[c, g].start()

    for c in range(len(CHUNKS)):
        all_of(stage[c], a_recv.at[c]).wait()
        if c in (2, 3):
            issue(c + 2)
        copies = []
        if c == 0:
            copies = [apply_left(c, g) for g in range(3)]
            combine(c, 0, copies[0])
            combine(c, 1, copies[1])
            lax.fori_loop(ASKING + BEFORE, blocks, mix, 0)
            combine(c, 2, copies[2])
            copies += [apply_left(c, g) for g in (3, 4)]
            combine(c, 3, copies[3])
            combine(c, 4, copies[4])
            issue(3)
        else:
            for g in range(len(PIECES[c])):
                copies.append(apply_left(c, g))
                if g:
                    combine(c, g - 1, copies[g - 1])
            combine(c, len(PIECES[c]) - 1, copies[-1])

    all_of(asked.at[pl.ds(0, OWNERS - 1)], tab_send).wait()
    for c in range(len(CHUNKS)):
        all_of(stage[c], a_send.at[c]).wait()
    for p in range(PHASES):
        all_of(give[p], g_send.at[p]).wait()
    for p in range(PHASES - 1):
        all_of(ring_out[p], n_send.at[p]).wait()


def on_device(psi, mpo, left_env, right_env, left_dims, right_dims, dest_owner, left_slot):
    blocks, states, width = psi.shape[0], psi.shape[1], psi.shape[2]
    sectors = left_env.shape[1]
    rows = width // (2 * Z)
    wide = states * width
    chunks = len(CHUNKS)
    hbm = pl.BlockSpec(memory_space=pl.ANY)
    dma = pltpu.SemaphoreType.DMA
    piece = pltpu.VMEM((blocks, rows, wide), BF16)
    return pl.pallas_call(
        kernel,
        out_shape=pltpu.VMEM((blocks, states, rows, width), BF16),
        in_specs=[hbm] * 8,
        out_specs=pl.BlockSpec(memory_space=pltpu.VMEM),
        scratch_shapes=[
            pltpu.SMEM(mpo.shape, F32),
            pltpu.SMEM((sectors,), jnp.int32),
            pltpu.SMEM((blocks,), jnp.int32),
            pltpu.SMEM((blocks,), jnp.int32),
            pltpu.SMEM((blocks,), jnp.int32),
            pltpu.VMEM((sectors, width, width), BF16),
            pltpu.VMEM((1, 128), jnp.int32),
            pltpu.SMEM((OWNERS, 1, 128), jnp.int32),
            pltpu.SMEM((blocks,), jnp.int32),
            *[pltpu.VMEM((OWNERS - 1, CAP, 2 * num, width), BF16) for _, _, num in CHUNKS],
            *[pltpu.VMEM((OWNERS * CAP, 2 * num, width), BF16) for _, _, num in CHUNKS],
            pltpu.VMEM((blocks, states, width, width), BF16),
            pltpu.VMEM((blocks, width, width), BF16),
            pltpu.VMEM((blocks, rows, wide), F32),
            *[piece] * (2 * PHASES + 2 * (PHASES - 1)),
            dma((5,)),
            dma,
            dma,
            dma,
            dma((chunks,)),
            dma((chunks,)),
            dma((blocks // PSI_READ,)),
            dma((blocks // RIGHT_READ,)),
            dma,
            dma((PHASES,)),
            dma((2, MOST)),
            dma((PHASES - 1,)),
            dma((chunks - 1, MOST)),
        ],
        compiler_params=pltpu.CompilerParams(
            collective_id=0, has_side_effects=True, vmem_limit_bytes=58 << 20
        ),
    )(mpo, left_dims, right_dims, dest_owner.reshape(blocks), left_slot, left_env, psi, right_env)


def solution(mesh):
    in_specs = (
        P("sec", None, None, None),
        P("chan", None, None),
        P("chan", "sec", None, None),
        P("chan", "sec", None, None),
        P("sec"),
        P("sec"),
        P("sec", None),
        P("sec"),
    )
    out_specs = P("sec", None, "chan", None)
    return jax.shard_map(
        on_device, mesh=mesh, in_specs=in_specs, out_specs=out_specs, check_vma=False
    )
```
